512 devices in a mesh: aux: 32 (over z, y_hi), pair: 16 (over x, y_lo, core).
Axes of the slice: x: 4, y: 4 (y_hi: 2, y_lo: 2; y = y_hi * 2 + y_lo), z: 16, core: 2. Of those that a mesh axis runs over, the one named last changes fastest.
Arguments:
- half_ints: bfloat16 [96, 1408, 4096], P('pair', None, 'aux'), may hold values from -0.75 to 0.75
- vir_coeffs: bfloat16 [1408, 1280], P(None, 'aux'), may hold values from -0.15625 to 0.15625
- occ_energy: float32 [96], replicated, may hold values from -2 to -0.3
- vir_energy: float32 [1280], replicated, may hold values from 0.3 to 4
- roster: int32 [32, 2], replicated, may hold values from 0 to 15
Outputs:
- density: bfloat16 [1280, 96, 4096], P('pair', 'aux')
The draws below stay inside these ranges and needn't reach their ends.
All inputs are finite; a program needn't handle non-finite values.
Results may differ from the reference program's by a relative error of at most 0.0058.
Values may be sent and summed in bfloat16 or wider, within the bound.
A program may use at most 64 MiB of HBM per device.

```python
import jax
import jax.numpy as jnp
from jax import lax

N = 1408
V = 1280
P_SIZE = 4096
OCC_BLK = 3
STEPS = 2
OCC = 96
VBLOCKS = 16
N_AUX = 32
N_PAIR = 16


def place_ends(array, rng, low, largest):
    place = [jax.random.randint(jax.random.fold_in(rng, axis), (), 0, length) for axis, length in enumerate(array.shape)]
    widest = array.shape.index(max(array.shape))
    next_to = place[:widest] + [(place[widest] + 1) % array.shape[widest]] + place[widest + 1:]
    return array.at[tuple(place)].set(low).at[tuple(next_to)].set(largest)


def level_of(rng, dims, cuts, low, top_value):
    factor_of = 1.0
    for dim, parts in cuts:
        steps = jax.random.uniform(jax.random.fold_in(jax.random.fold_in(rng, 6), dim), (parts,), jnp.float32, low / len(cuts), top_value / len(cuts))
        factor_of = factor_of * jnp.repeat(jnp.exp(steps), dims[dim] // parts).reshape((-1,) + (1,) * (len(dims) - 1 - dim))
    return factor_of


def normal_values(stream_key, shape, scale, reach, cuts=(), kind=jnp.bfloat16):
    factor_of = level_of(stream_key, shape, cuts, -0.22, 0.18) if cuts else 1.0
    values = jax.random.normal(stream_key, shape, jnp.float32) * scale * factor_of
    return jnp.minimum(jnp.maximum(values, -reach), reach).astype(kind)


def setup_inputs(seed: int = 0) -> dict:
    splits = jax.random.split(jax.random.key(seed), 6)
    half_ints = normal_values(splits[0], (OCC, N, P_SIZE), 0.125, 0.75, ((0, 16), (2, 32)))
    vir_coeffs = normal_values(splits[1], (N, V), N ** -0.5, 0.15625, ((1, 32),))
    occ_energy = jnp.clip(jax.random.uniform(splits[2], (OCC,), jnp.float32, -2.0, -0.3), -2.0, -0.3)
    vir_energy = jnp.clip(jax.random.uniform(splits[3], (V,), jnp.float32, 0.3, 4.0), 0.3, 4.0)
    roster = place_ends(jax.random.randint(splits[4], (OCC // OCC_BLK, STEPS), 0, VBLOCKS), jax.random.fold_in(splits[4], 1), 0, VBLOCKS - 1).astype(jnp.int32)
    return dict(half_ints=half_ints, vir_coeffs=vir_coeffs, occ_energy=occ_energy, vir_energy=vir_energy, roster=roster)


spin_scale = 1.3


def reference(half_ints, vir_coeffs, occ_energy, vir_energy, roster):
    vir_width = V // N_PAIR
    coeff_rows = jnp.transpose(vir_coeffs)

    def one_block(block_index):
        row_start = (block_index * OCC_BLK).astype(jnp.int32)
        half_block = lax.dynamic_slice_in_dim(half_ints, row_start, OCC_BLK, 0)
        half_flat = jnp.transpose(half_block, (1, 0, 2)).reshape(N, OCC_BLK * P_SIZE)
        vir_ints = jnp.dot(coeff_rows, half_flat, preferred_element_type=jnp.float32).astype(jnp.bfloat16).reshape(V, OCC_BLK, P_SIZE)
        occ_block = lax.dynamic_slice_in_dim(occ_energy, row_start, OCC_BLK, 0)
        flat_local = vir_ints.reshape(V * OCC_BLK, P_SIZE)
        energy_left = (vir_energy[:, None] - occ_block[None, :]).reshape(-1)
        block_plan = lax.dynamic_index_in_dim(roster, block_index, 0, keepdims=False)

        def pair_step(density, source):
            first_row = (source * vir_width).astype(jnp.int32)
            flat_remote = lax.dynamic_slice_in_dim(vir_ints, first_row, vir_width, 0).reshape(vir_width * OCC_BLK, P_SIZE)
            energy_block = lax.dynamic_slice_in_dim(vir_energy, first_row, vir_width, 0)
            energy_right = (energy_block[:, None] - occ_block[None, :]).reshape(-1)
            integrals = jnp.dot(flat_local, jnp.transpose(flat_remote), preferred_element_type=jnp.float32)
            amplitudes = (spin_scale * integrals / (energy_left[:, None] + energy_right[None, :])).astype(jnp.bfloat16)
            return density + jnp.dot(amplitudes, flat_remote, preferred_element_type=jnp.float32), None

        density, unused = lax.scan(pair_step, jnp.zeros((V * OCC_BLK, P_SIZE), jnp.float32), block_plan)
        return density.astype(jnp.bfloat16).reshape(V, OCC_BLK, P_SIZE)

    blocks = lax.map(one_block, jnp.arange(N_AUX, dtype=jnp.int32))
    return jnp.transpose(blocks, (1, 0, 2, 3)).reshape(V, N_AUX * OCC_BLK, P_SIZE)
```

```python
import jax
import jax.numpy as jnp
from jax import lax
from jax.experimental import pallas as pl
from jax.experimental.pallas import tpu as pltpu
from jax.sharding import PartitionSpec as P

spin_scale = 1.3
MESH = pl.DeviceIdType.MESH
ANY = pl.BlockSpec(memory_space=pl.ANY)
DMA = pltpu.SemaphoreType.DMA

GROUP = 384


def place():
    aux, pair = lax.axis_index("aux"), lax.axis_index("pair")
    return aux // 2, aux % 2, pair // 4, (pair // 2) % 2, pair % 2, aux, pair


def chip_of(c):
    return c // 8, (c // 4) % 2, c % 4


def remote(src, dst, send, recv, device):
    return pltpu.make_async_remote_copy(
        src_ref=src, dst_ref=dst, send_sem=send, recv_sem=recv,
        device_id=device, device_id_type=MESH,
    )


def signal(device):
    pl.semaphore_signal(
        pltpu.get_barrier_semaphore(), inc=1, device_id=device, device_id_type=MESH
    )


def gather_kernel(src, out, own_sem, send_z, recv_z, send_p, recv_p, send_c, recv_c):
    z, h, x, yl, core, aux, pair = place()
    w = yl * 2 + core
    chip = (h * 2 + yl) * 4 + x
    partner = (aux, pair + 1 - 2 * core)

    def z_peer(d):
        return (((z + d) % 16) * 2 + h, pair)

    def chip_peer(e):
        ph, pyl, px = chip_of((chip + e) % 16)
        return (z * 2 + ph, px * 4 + pyl * 2 + core)

    def region(c, at_core):
        ch, cyl, cx = chip_of(c)
        columns = pl.ds(pl.multiple_of(cx * GROUP, 128), GROUP)
        return out.at[:, (cyl * 2 + at_core) * 2 + ch, :, columns]

    @pl.loop(1, 16)
    def _(d):
        signal(z_peer(d))
        signal(chip_peer(d))

    signal(partner)
    pl.semaphore_wait(pltpu.get_barrier_semaphore(), 31)

    mine = pl.ds(pl.multiple_of(x * GROUP, 128), GROUP)

    def slot(t):
        return out.at[t, w * 2 + h, :, mine]

    owner = z % 4 == w

    @pl.when(owner)
    def _():
        @pl.loop(1, 16)
        def _(d):
            remote(src.at[:, mine], slot(z // 4), send_z.at[d], recv_z.at[z // 4], z_peer(d)).start()

        copy = pltpu.make_async_copy(src.at[:, mine], slot(z // 4), own_sem)
        copy.start()
        copy.wait()

    @pl.loop(0, 4)
    def _(t):
        @pl.when(jnp.logical_or(jnp.logical_not(owner), t != z // 4))
        def _():
            remote(slot(t), slot(t), send_z.at[0], recv_z.at[t], partner).wait_recv()

    @pl.loop(1, 16)
    def _(e):
        remote(region(chip, core), region(chip, core), send_p.at[e], recv_p.at[chip], chip_peer(e)).start()

    remote(region(chip, core), region(chip, core), send_c.at[chip], recv_c.at[chip], partner).start()

    @pl.loop(1, 16)
    def _(e):
        c = (chip + 16 - e) % 16
        part = region(c, core)
        remote(part, part, send_c.at[c], recv_p.at[c], partner).wait_recv()
        remote(part, part, send_c.at[c], recv_c.at[c], partner).start()

    @pl.loop(0, 16)
    def _(c):
        part = region(c, 1 - core)
        remote(part, part, send_c.at[c], recv_c.at[c], partner).wait()

    @pl.loop(1, 16)
    def _(e):
        part = region(chip, core)
        remote(part, part, send_p.at[e], recv_p.at[chip], chip_peer(e)).wait_send()

    @pl.when(owner)
    def _():
        @pl.loop(1, 16)
        def _(d):
            remote(src.at[:, mine], slot(z // 4), send_z.at[d], recv_z.at[0], z_peer(d)).wait_send()


def gather_columns(rows):
    return pl.pallas_call(
        gather_kernel,
        out_shape=jax.ShapeDtypeStruct((4, 8) + rows.shape, rows.dtype),
        in_specs=[ANY],
        out_specs=ANY,
        scratch_shapes=[DMA, DMA((16,)), DMA((4,)), DMA((16,)), DMA((16,)), DMA((16,)), DMA((16,))],
        compiler_params=pltpu.CompilerParams(collective_id=0, has_side_effects=True),
        name="gather_columns",
    )(rows)


def transform_kernel(coeff, half, out):
    wide = jnp.concatenate([half[i] for i in range(6)], axis=1)
    product = jnp.dot(coeff[...], wide, preferred_element_type=jnp.float32)
    product = product.astype(jnp.bfloat16)
    for v in range(out.shape[0]):
        for i in range(6):
            out[v, i // 3, i % 3] = product[80 * v : 80 * v + 80, 128 * i : 128 * i + 128]


def transform(coeff, half):
    steps = 4
    rows = 1280 // steps
    return pl.pallas_call(
        transform_kernel,
        out_shape=jax.ShapeDtypeStruct((16, 2, 3, 80, 128), jnp.bfloat16),
        grid=(steps,),
        in_specs=[
            pl.BlockSpec((rows, 1408), lambda g: (g, 0)),
            pl.BlockSpec((6, 1408, 128), lambda g: (0, 0, 0)),
        ],
        out_specs=pl.BlockSpec((16 // steps, 2, 3, 80, 128), lambda g: (g, 0, 0, 0, 0)),
        name="transform",
    )(coeff, half)


def select_kernel(plan, block, out):
    out[0] = block[0, 0]


def select(plan, vir):
    return pl.pallas_call(
        select_kernel,
        out_shape=jax.ShapeDtypeStruct((2, 6, 80, 128), jnp.bfloat16),
        grid_spec=pltpu.PrefetchScalarGridSpec(
            num_scalar_prefetch=1,
            grid=(2, 2),
            in_specs=[pl.BlockSpec((1, 1, 3, 80, 128), lambda h, s, plan: (plan[h, s], h, 0, 0, 0))],
            out_specs=pl.BlockSpec((1, 3, 80, 128), lambda h, s, plan: (h, s, 0, 0)),
        ),
        name="select",
    )(plan, vir)


def exchange_kernel(
    vir, chosen, local, paired, relay, relay_r, own_sem, send_v, recv_v, send_w, recv_w,
    send_x, recv_x, send_r, recv_r, send_g, recv_g, send_c, recv_c,
):
    z, h, x, yl, core, aux, pair = place()
    partner = (aux, pair + 1 - 2 * core)
    own = pl.ds(pl.multiple_of(aux * 128, 128), 128)
    q_own = pair // 2

    @pl.loop(1, 16)
    def _(d):
        signal((aux, (pair + d) % 16))

    @pl.loop(1, 32)
    def _(d):
        signal(((aux + d) % 32, pair))

    pl.semaphore_wait(pltpu.get_barrier_semaphore(), 46)

    def chip_pair(q):
        return q * 2 + core

    def spread(q, at_core):
        first = (q * 2 + at_core + 16 - z) % 16
        return paired.at[:, :, pl.ds(pl.multiple_of(first * 256, 128), 256)]

    def chosen_out():
        return remote(chosen, relay_r, send_w, recv_w, (aux, (pair + z) % 16))

    @pl.when(z != 0)
    def _():
        chosen_out().start()

    def vir_out(n):
        v = (pair + n) % 16
        return remote(vir.at[v], relay.at[pair], send_v.at[n], recv_v.at[pair], (aux, v))

    @pl.loop(0, 16)
    def _(n):
        turn = (n + z) % 16

        @pl.when(turn != 0)
        def _():
            vir_out(turn).start()

    def onward(src, dst, send, recv, plane, to_h, home_sem):
        at_home = jnp.logical_and(plane == z, to_h == h)

        @pl.when(at_home)
        def _():
            pltpu.make_async_copy(src, dst, home_sem).start()

        @pl.when(jnp.logical_not(at_home))
        def _():
            remote(src, dst, send, recv, (plane * 2 + to_h, pair)).start()

    plane_r = (pair + 16 - z) % 16

    def chosen_on(src):
        @pl.loop(0, 2)
        def _(to_h):
            onward(src.at[to_h], paired.at[:, :, own], send_r.at[to_h], recv_r.at[h], plane_r, to_h, own_sem.at[0])

    @pl.when(z == 0)
    def _():
        chosen_on(chosen)

    @pl.when(z != 0)
    def _():
        chosen_out().wait_recv()
        chosen_on(relay_r)

    @pl.loop(0, 16)
    def _(n):
        turn = (n + z) % 16
        plane = (pair + 16 - turn) % 16

        def forward(src):
            @pl.loop(0, 2)
            def _(to_h):
                onward(
                    src.at[to_h], local.at[:, :, own], send_x.at[plane * 2 + to_h],
                    recv_x.at[aux], plane, to_h, own_sem.at[1],
                )

        @pl.when(turn == 0)
        def _():
            forward(vir.at[pair])

        @pl.when(turn != 0)
        def _():
            remote(relay.at[plane], relay.at[plane], send_v.at[0], recv_v.at[plane], partner).wait_recv()
            forward(relay.at[plane])

    @pl.loop(0, 2)
    def _(from_h):
        home = jnp.logical_and(plane_r == z, from_h == h)
        first = (pair + 16 - z) % 16
        part = paired.at[:, :, pl.ds(pl.multiple_of((first * 2 + from_h) * 128, 128), 128)]

        @pl.when(home)
        def _():
            pltpu.make_async_copy(chosen.at[0], part, own_sem.at[0]).wait()

        @pl.when(jnp.logical_not(home))
        def _():
            remote(part, part, send_r.at[0], recv_r.at[from_h], partner).wait_recv()

    mine = spread(q_own, core)

    @pl.loop(1, 8)
    def _(e):
        remote(mine, mine, send_g.at[e], recv_g.at[q_own], (aux, chip_pair((q_own + e) % 8))).start()

    remote(mine, mine, send_c.at[q_own], recv_c.at[q_own], partner).start()

    @pl.loop(1, 8)
    def _(e):
        q = (q_own + 8 - e) % 8
        part = spread(q, core)
        remote(part, part, send_c.at[q], recv_g.at[q], partner).wait_recv()
        remote(part, part, send_c.at[q], recv_c.at[q], partner).start()

    @pl.loop(0, 8)
    def _(q):
        part = spread(q, 1 - core)
        remote(part, part, send_c.at[q], recv_c.at[q], partner).wait()

    @pl.loop(1, 8)
    def _(e):
        remote(mine, mine, send_g.at[e], recv_g.at[q_own], (aux, chip_pair((q_own + e) % 8))).wait_send()

    @pl.when(z != 0)
    def _():
        chosen_out().wait_send()

    @pl.loop(1, 16)
    def _(n):
        vir_out(n).wait_send()

    @pl.loop(0, 2)
    def _(to_h):
        @pl.when(jnp.logical_not(jnp.logical_and(plane_r == z, to_h == h)))
        def _():
            part = paired.at[:, :, own]
            remote(chosen.at[to_h], part, send_r.at[to_h], recv_r.at[0], partner).wait_send()

    @pl.loop(0, 32)
    def _(a):
        part = local.at[:, :, pl.ds(pl.multiple_of(a * 128, 128), 128)]

        @pl.when(a == aux)
        def _():
            pltpu.make_async_copy(vir.at[0, 0], part, own_sem.at[1]).wait()

        @pl.when(a != aux)
        def _():
            remote(vir.at[0, 0], part, send_x.at[a], recv_x.at[a], partner).wait()


def exchange(vir, chosen):
    return pl.pallas_call(
        exchange_kernel,
        out_shape=(
            jax.ShapeDtypeStruct((3, 80, 4096), jnp.bfloat16),
            jax.ShapeDtypeStruct((6, 80, 4096), jnp.bfloat16),
        ),
        in_specs=[ANY, ANY],
        out_specs=(ANY, ANY),
        scratch_shapes=[
            pltpu.VMEM((16, 2, 3, 80, 128), jnp.bfloat16),
            pltpu.VMEM((2, 6, 80, 128), jnp.bfloat16),
            DMA((2,)), DMA((16,)), DMA((16,)), DMA, DMA,
            DMA((32,)), DMA((32,)), DMA((2,)), DMA((2,)),
            DMA((8,)), DMA((8,)), DMA((8,)), DMA((8,)),
        ],
        compiler_params=pltpu.CompilerParams(collective_id=1, has_side_effects=True),
        name="exchange",
    )(vir, chosen)


def per_device(half_ints, vir_coeffs, occ_energy, vir_energy, roster):
    aux, pair = lax.axis_index("aux"), lax.axis_index("pair")
    rows = jnp.pad(jnp.transpose(vir_coeffs), ((0, 0), (0, 4 * GROUP - vir_coeffs.shape[0])))
    columns = gather_columns(rows).reshape(1280, 4 * GROUP)
    vir = transform(columns, half_ints)
    plan = lax.dynamic_slice_in_dim(roster, pair * 2, 2, 0)
    local, paired = exchange(vir, select(plan, vir))
    flat_local = local.reshape(240, 4096)
    paired = paired.reshape(2, 240, 4096)
    occ_block = lax.dynamic_slice_in_dim(occ_energy, aux * 3, 3, 0)
    vir_block = lax.dynamic_slice_in_dim(vir_energy, pair * 80, 80, 0)
    energy_left = (vir_block[None, :] - occ_block[:, None]).reshape(-1)
    block_plan = lax.dynamic_index_in_dim(roster, aux, 0, keepdims=False)
    density = jnp.zeros((240, 4096), jnp.float32)
    for step in range(2):
        energy_block = lax.dynamic_slice_in_dim(vir_energy, block_plan[step] * 80, 80, 0)
        energy_right = (energy_block[None, :] - occ_block[:, None]).reshape(-1)
        integrals = lax.dot_general(
            flat_local, paired[step], (((1,), (1,)), ((), ())), preferred_element_type=jnp.float32
        )
        amplitudes = (
            spin_scale * integrals / (energy_left[:, None] + energy_right[None, :])
        ).astype(jnp.bfloat16)
        density = density + jnp.dot(amplitudes, paired[step], preferred_element_type=jnp.float32)
    return jnp.transpose(density.astype(jnp.bfloat16).reshape(3, 80, 4096), (1, 0, 2))


def solution(mesh):
    in_specs = (P("pair", None, "aux"), P(None, "aux"), P(), P(), P())
    out_specs = P("pair", "aux", None)
    return jax.shard_map(
        per_device, mesh=mesh, in_specs=in_specs, out_specs=out_specs, check_vma=False
    )
```

```python
import jax
import jax.numpy as jnp
from jax import lax
from jax.experimental import pallas as pl
from jax.experimental.pallas import tpu as pltpu
from jax.sharding import PartitionSpec as P

spin_scale = 1.3
MESH = pl.DeviceIdType.MESH
ANY = pl.BlockSpec(memory_space=pl.ANY)
DMA = pltpu.SemaphoreType.DMA

GROUP = 384


def place():
    aux, pair = lax.axis_index("aux"), lax.axis_index("pair")
    return aux // 2, aux % 2, pair // 4, (pair // 2) % 2, pair % 2, aux, pair


def remote(src, dst, send, recv, device):
    return pltpu.make_async_remote_copy(
        src_ref=src, dst_ref=dst, send_sem=send, recv_sem=recv,
        device_id=device, device_id_type=MESH,
    )


def signal(device):
    pl.semaphore_signal(
        pltpu.get_barrier_semaphore(), inc=1, device_id=device, device_id_type=MESH
    )


def front_kernel(
    plan, rows, half_hbm, local, paired, columns, half, coeff, vir, relay, chosen, relay_r,
    half_sem, own_sem, home_sem, send_z, recv_z, send_p, recv_p, send_k, recv_k,
    send_v, recv_v, send_w, recv_w, send_x, recv_x, send_r, recv_r, send_g, recv_g, send_c, recv_c,
):
    z, h, x, yl, core, aux, pair = place()
    w = yl * 2 + core
    side = h * 4 + x
    partner = (aux, pair + 1 - 2 * core)
    own = pl.ds(pl.multiple_of(aux * 128, 128), 128)
    q_own = pair // 2

    half_load = pltpu.make_async_copy(half_hbm, half, half_sem)
    half_load.start()

    @pl.loop(1, 16)
    def _(d):
        signal((aux, (pair + d) % 16))

    @pl.loop(1, 32)
    def _(d):
        signal(((aux + d) % 32, pair))

    @pl.loop(1, 8)
    def _(d):
        signal((z * 2 + 1 - h, ((q_own + d) % 8) * 2 + core))

    pl.semaphore_wait(pltpu.get_barrier_semaphore(), 53)

    def z_peer(d):
        return (((z + d) % 16) * 2 + h, pair)

    def piece(ch, cyl, cx, at_core, t):
        first = pl.multiple_of((8 * t + 2 * (cyl * 2 + at_core) + ch) * 40, 8)
        return columns.at[pl.ds(first, 40), pl.ds(pl.multiple_of(cx * GROUP, 128), GROUP)]

    def mine(t):
        return piece(h, yl, x, core, t)

    row_part = rows.at[:, pl.ds(pl.multiple_of(x * GROUP, 128), GROUP)]
    owner = z % 4 == w

    @pl.when(owner)
    def _():
        @pl.loop(1, 16)
        def _(d):
            remote(row_part, mine(z // 4), send_z.at[d], recv_z.at[z // 4], z_peer(d)).start()

        copy = pltpu.make_async_copy(row_part, mine(z // 4), home_sem.at[0])
        copy.start()
        copy.wait()

    def to_chip(e, t):
        other = (side + e) % 8
        device = (z * 2 + other // 4, (other % 4) * 4 + ((yl + e // 8) % 2) * 2 + core)
        return remote(mine(t), mine(t), send_p.at[e, t], recv_p.at[yl * 8 + side, t], device)

    def to_partner(cyl, cside, t):
        part = piece(cside // 4, cyl, cside % 4, core, t)
        return remote(part, part, send_k.at[cyl * 8 + cside, t], recv_k.at[cyl * 8 + cside, t], partner)

    @pl.loop(0, 4)
    def _(t):
        @pl.when(jnp.logical_or(jnp.logical_not(owner), t != z // 4))
        def _():
            remote(mine(t), mine(t), send_z.at[0], recv_z.at[t], partner).wait_recv()

        @pl.loop(1, 8)
        def _(e):
            to_chip(e, t).start()

        to_partner(yl, side, t).start()

    @pl.loop(0, 4)
    def _(t):
        @pl.loop(8, 16)
        def _(e):
            to_chip(e, t).start()

    half_load.wait()

    def vir_out(v):
        return remote(vir.at[v], relay.at[pair], send_v.at[v], recv_v.at[pair], (aux, v))

    def turn_of(g):
        return (w + (1 - 2 * core) * (g // 2) + 2 * (g % 2)) % 4

    def onward(src, dst, send, recv, plane, to_h, sem):
        at_home = jnp.logical_and(plane == z, to_h == h)

        @pl.when(at_home)
        def _():
            pltpu.make_async_copy(src, dst, sem).start()

        @pl.when(jnp.logical_not(at_home))
        def _():
            remote(src, dst, send, recv, (plane * 2 + to_h, pair)).start()

    def forward(g):
        @pl.loop(0, 4)
        def _(n):
            plane = ((x + n + z) % 4) * 4 + turn_of(g)

            def both(src):
                @pl.loop(0, 2)
                def _(to_h):
                    onward(
                        src.at[to_h], local.at[:, :, own], send_x.at[plane * 2 + to_h],
                        recv_x.at[aux], plane, to_h, home_sem.at[1],
                    )

            @pl.when(plane == pair)
            def _():
                both(vir.at[pair])

            @pl.when(plane != pair)
            def _():
                remote(relay.at[plane], relay.at[plane], send_v.at[0], recv_v.at[plane], partner).wait_recv()
                both(relay.at[plane])

    @pl.loop(0, 4)
    def _(g):
        w_now = turn_of(g)
        yl_now = (yl + g % 2) % 2

        @pl.loop(0, 8)
        def _(other):
            @pl.loop(0, 4)
            def _(t):
                @pl.when(jnp.logical_and(g < 2, jnp.logical_or(g == 1, other != side)))
                def _():
                    part = piece(other // 4, yl_now, other % 4, core, t)
                    remote(part, part, send_p.at[0, 0], recv_p.at[yl_now * 8 + other, t], partner).wait_recv()
                    to_partner(yl_now, other, t).start()

                @pl.when(g >= 2)
                def _():
                    part = piece(other // 4, yl_now, other % 4, 1 - core, t)
                    remote(part, part, send_p.at[0, 0], recv_k.at[yl_now * 8 + other, t], partner).wait_recv()

        def load(t):
            first = pl.multiple_of((4 * t + w_now) * 80, 16)
            return pltpu.make_async_copy(columns.at[pl.ds(first, 80), pl.ds(0, 1408)], coeff.at[t], own_sem.at[t])

        for t in range(4):
            load(t).start()
        for t in range(4):
            load(t).wait()
        wide = jnp.concatenate([half[i] for i in range(6)], axis=1)
        product = jnp.dot(coeff[...].reshape(320, 1408), wide, preferred_element_type=jnp.float32)
        product = product.astype(jnp.bfloat16)
        for t in range(4):
            for i in range(6):
                vir[4 * t + w_now, i // 3, i % 3] = product[80 * t : 80 * t + 80, 128 * i : 128 * i + 128]

        @pl.loop(0, 4)
        def _(n):
            v = ((x + n + 4 - z % 4) % 4) * 4 + w_now

            @pl.when(v != pair)
            def _():
                vir_out(v).start()

        @pl.when(g == 0)
        def _():
            forward(0)

    for to_h in range(2):
        for step in range(2):
            chosen[to_h, 3 * step : 3 * step + 3] = vir[plan[to_h, step], to_h]

    def chosen_out():
        return remote(chosen, relay_r, send_w, recv_w, (aux, (pair + z) % 16))

    plane_r = (pair + 16 - z) % 16

    def chosen_on(src):
        @pl.loop(0, 2)
        def _(to_h):
            onward(src.at[to_h], paired.at[:, :, own], send_r.at[to_h], recv_r.at[h], plane_r, to_h, home_sem.at[0])

    @pl.when(z == 0)
    def _():
        chosen_on(chosen)

    @pl.when(z != 0)
    def _():
        chosen_out().start()
        chosen_out().wait_recv()
        chosen_on(relay_r)

    @pl.loop(1, 4)
    def _(g):
        forward(g)

    def spread(q, at_core):
        first = (q * 2 + at_core + 16 - z) % 16
        return paired.at[:, :, pl.ds(pl.multiple_of(first * 256, 128), 256)]

    def spread_out(e):
        part = spread(q_own, core)
        return remote(part, part, send_g.at[e], recv_g.at[q_own], (aux, ((q_own + e) % 8) * 2 + core))

    @pl.loop(0, 2)
    def _(from_h):
        home = jnp.logical_and(plane_r == z, from_h == h)
        part = paired.at[:, :, pl.ds(pl.multiple_of((plane_r * 2 + from_h) * 128, 128), 128)]

        @pl.when(home)
        def _():
            pltpu.make_async_copy(chosen.at[0], part, home_sem.at[0]).wait()

        @pl.when(jnp.logical_not(home))
        def _():
            remote(part, part, send_r.at[0], recv_r.at[from_h], partner).wait_recv()

    @pl.loop(1, 8)
    def _(e):
        spread_out(e).start()

    part = spread(q_own, core)
    remote(part, part, send_c.at[q_own], recv_c.at[q_own], partner).start()

    @pl.loop(1, 8)
    def _(e):
        q = (q_own + 8 - e) % 8
        part = spread(q, core)
        remote(part, part, send_c.at[q], recv_g.at[q], partner).wait_recv()
        remote(part, part, send_c.at[q], recv_c.at[q], partner).start()

    @pl.loop(0, 8)
    def _(q):
        part = spread(q, 1 - core)
        remote(part, part, send_c.at[q], recv_c.at[q], partner).wait()

    @pl.loop(1, 8)
    def _(e):
        spread_out(e).wait_send()

    @pl.when(owner)
    def _():
        @pl.loop(1, 16)
        def _(d):
            remote(row_part, mine(z // 4), send_z.at[d], recv_z.at[0], z_peer(d)).wait_send()

    @pl.loop(0, 4)
    def _(t):
        @pl.loop(1, 16)
        def _(e):
            to_chip(e, t).wait_send()

        @pl.loop(0, 16)
        def _(c):
            to_partner(c // 8, c % 8, t).wait_send()

    @pl.when(z != 0)
    def _():
        chosen_out().wait_send()

    @pl.loop(0, 16)
    def _(v):
        @pl.when(v != pair)
        def _():
            vir_out(v).wait_send()

    @pl.loop(0, 2)
    def _(to_h):
        @pl.when(jnp.logical_not(jnp.logical_and(plane_r == z, to_h == h)))
        def _():
            part = paired.at[:, :, own]
            remote(chosen.at[to_h], part, send_r.at[to_h], recv_r.at[0], partner).wait_send()

    @pl.loop(0, 32)
    def _(a):
        part = local.at[:, :, pl.ds(pl.multiple_of(a * 128, 128), 128)]

        @pl.when(a == aux)
        def _():
            pltpu.make_async_copy(vir.at[0, 0], part, home_sem.at[1]).wait()

        @pl.when(a != aux)
        def _():
            remote(vir.at[0, 0], part, send_x.at[a], recv_x.at[a], partner).wait()


def front(plan, rows, half):
    bf16 = jnp.bfloat16
    return pl.pallas_call(
        front_kernel,
        out_shape=(
            jax.ShapeDtypeStruct((3, 80, 4096), bf16),
            jax.ShapeDtypeStruct((6, 80, 4096), bf16),
            jax.ShapeDtypeStruct((1280, 4 * GROUP), bf16),
        ),
        in_specs=[pl.BlockSpec(memory_space=pltpu.SMEM), ANY, ANY],
        out_specs=(ANY, ANY, ANY),
        scratch_shapes=[
            pltpu.VMEM((6, 1408, 128), bf16),
            pltpu.VMEM((4, 80, 1408), bf16),
            pltpu.VMEM((16, 2, 3, 80, 128), bf16),
            pltpu.VMEM((16, 2, 3, 80, 128), bf16),
            pltpu.VMEM((2, 6, 80, 128), bf16),
            pltpu.VMEM((2, 6, 80, 128), bf16),
            DMA, DMA((4,)), DMA((2,)),
            DMA((16,)), DMA((4,)), DMA((16, 4)), DMA((16, 4)), DMA((16, 4)), DMA((16, 4)),
            DMA((16,)), DMA((16,)), DMA, DMA,
            DMA((32,)), DMA((32,)), DMA((2,)), DMA((2,)),
            DMA((8,)), DMA((8,)), DMA((8,)), DMA((8,)),
        ],
        compiler_params=pltpu.CompilerParams(collective_id=0, has_side_effects=True),
        name="front",
    )(plan, rows, half)


def per_device(half_ints, vir_coeffs, occ_energy, vir_energy, roster):
    aux, pair = lax.axis_index("aux"), lax.axis_index("pair")
    rows = jnp.pad(jnp.transpose(vir_coeffs), ((0, 0), (0, 4 * GROUP - vir_coeffs.shape[0])))
    plan = lax.dynamic_slice_in_dim(roster, pair * 2, 2, 0)
    local, paired, _ = front(plan, rows, half_ints)
    flat_local = local.reshape(240, 4096)
    paired = paired.reshape(2, 240, 4096)
    occ_block = lax.dynamic_slice_in_dim(occ_energy, aux * 3, 3, 0)
    vir_block = lax.dynamic_slice_in_dim(vir_energy, pair * 80, 80, 0)
    energy_left = (vir_block[None, :] - occ_block[:, None]).reshape(-1)
    block_plan = lax.dynamic_index_in_dim(roster, aux, 0, keepdims=False)
    density = jnp.zeros((240, 4096), jnp.float32)
    for step in range(2):
        energy_block = lax.dynamic_slice_in_dim(vir_energy, block_plan[step] * 80, 80, 0)
        energy_right = (energy_block[None, :] - occ_block[:, None]).reshape(-1)
        integrals = lax.dot_general(
            flat_local, paired[step], (((1,), (1,)), ((), ())), preferred_element_type=jnp.float32
        )
        amplitudes = (
            spin_scale * integrals / (energy_left[:, None] + energy_right[None, :])
        ).astype(jnp.bfloat16)
        density = density + jnp.dot(amplitudes, paired[step], preferred_element_type=jnp.float32)
    return jnp.transpose(density.astype(jnp.bfloat16).reshape(3, 80, 4096), (1, 0, 2))


def solution(mesh):
    in_specs = (P("pair", None, "aux"), P(None, "aux"), P(), P(), P())
    out_specs = P("pair", "aux", None)
    return jax.shard_map(
        per_device, mesh=mesh, in_specs=in_specs, out_specs=out_specs, check_vma=False
    )
```

```python
import jax
import jax.numpy as jnp
from jax import lax
from jax.experimental import pallas as pl
from jax.experimental.pallas import tpu as pltpu
from jax.sharding import PartitionSpec as P

spin_scale = 1.3
MESH = pl.DeviceIdType.MESH
ANY = pl.BlockSpec(memory_space=pl.ANY)
DMA = pltpu.SemaphoreType.DMA

GROUP = 384


def place():
    aux, pair = lax.axis_index("aux"), lax.axis_index("pair")
    return aux // 2, aux % 2, pair // 4, (pair // 2) % 2, pair % 2, aux, pair


def remote(src, dst, send, recv, device):
    return pltpu.make_async_remote_copy(
        src_ref=src, dst_ref=dst, send_sem=send, recv_sem=recv,
        device_id=device, device_id_type=MESH,
    )


def signal(device):
    pl.semaphore_signal(
        pltpu.get_barrier_semaphore(), inc=1, device_id=device, device_id_type=MESH
    )


def front_kernel(
    plan, rows, half_hbm, local, paired, columns, half, coeff, vir, relay, chosen, relay_r,
    half_sem, own_sem, home_sem, send_z, recv_z, send_p, recv_p, send_k, recv_k,
    send_v, recv_v, send_w, recv_w, send_x, recv_x, send_r, recv_r, send_g, recv_g, send_c, recv_c,
):
    z, h, x, yl, core, aux, pair = place()
    w = yl * 2 + core
    side = h * 4 + x
    partner = (aux, pair + 1 - 2 * core)
    q_own = pair // 2

    half_load = pltpu.make_async_copy(half_hbm, half, half_sem)
    half_load.start()

    @pl.loop(1, 16)
    def _(d):
        signal((((z + d) % 16) * 2 + h, pair))

    @pl.loop(1, 32)
    def _(d):
        other = (h * 16 + pair + d) % 32
        signal((z * 2 + other // 16, other % 16))

    pl.semaphore_wait(pltpu.get_barrier_semaphore(), 46)

    def z_peer(d):
        return (((z + d) % 16) * 2 + h, pair)

    def piece(ch, cyl, cx, at_core, t):
        first = pl.multiple_of((8 * t + 2 * (cyl * 2 + at_core) + ch) * 40, 8)
        return columns.at[pl.ds(first, 40), pl.ds(pl.multiple_of(cx * GROUP, 128), GROUP)]

    def mine(t):
        return piece(h, yl, x, core, t)

    row_part = rows.at[:, pl.ds(pl.multiple_of(x * GROUP, 128), GROUP)]
    owner = z % 4 == w

    @pl.when(owner)
    def _():
        @pl.loop(1, 16)
        def _(d):
            remote(row_part, mine(z // 4), send_z.at[d], recv_z.at[z // 4], z_peer(d)).start()

        copy = pltpu.make_async_copy(row_part, mine(z // 4), home_sem.at[0])
        copy.start()
        copy.wait()

    def to_chip(e, t):
        other = (side + e) % 8
        device = (z * 2 + other // 4, (other % 4) * 4 + ((yl + e // 8) % 2) * 2 + core)
        return remote(mine(t), mine(t), send_p.at[e, t], recv_p.at[yl * 8 + side, t], device)

    def to_partner(cyl, cside, t):
        part = piece(cside // 4, cyl, cside % 4, core, t)
        return remote(part, part, send_k.at[cyl * 8 + cside, t], recv_k.at[cyl * 8 + cside, t], partner)

    @pl.loop(0, 4)
    def _(t):
        @pl.when(jnp.logical_or(jnp.logical_not(owner), t != z // 4))
        def _():
            remote(mine(t), mine(t), send_z.at[0], recv_z.at[t], partner).wait_recv()

        @pl.loop(1, 8)
        def _(e):
            to_chip(e, t).start()

        to_partner(yl, side, t).start()

    half_load.wait()

    def vir_out(v, to_h):
        return remote(
            vir.at[v, to_h], relay.at[h, pair], send_v.at[v, to_h], recv_v.at[h, pair], (z * 2 + to_h, v)
        )

    def stays(v, to_h):
        return jnp.logical_and(v == pair, to_h == h)

    def turn_of(g):
        return (w + (1 - 2 * core) * (g // 2) + 2 * (g % 2)) % 4

    def q_of(array, a):
        return array.at[:, :, pl.ds(pl.multiple_of(a * 128, 128), 128)]

    def onward(src, dst, send, recv, plane, sem):
        @pl.when(plane == z)
        def _():
            pltpu.make_async_copy(src, dst, sem).start()

        @pl.when(plane != z)
        def _():
            remote(src, dst, send, recv, (plane * 2 + h, pair)).start()

    def vir_on(src, plane, from_h):
        a = z * 2 + from_h
        onward(src, q_of(local, a), send_x.at[plane, from_h], recv_x.at[a], plane, home_sem.at[from_h])

    def forward(g):
        @pl.loop(0, 8)
        def _(n):
            plane = ((x + n // 2 + z) % 4) * 4 + turn_of(g)
            from_h = n % 2

            @pl.when(stays(plane, from_h))
            def _():
                vir_on(vir.at[pair, h], plane, from_h)

            @pl.when(jnp.logical_not(stays(plane, from_h)))
            def _():
                block = relay.at[from_h, plane]
                remote(block, block, send_v.at[0, 0], recv_v.at[from_h, plane], partner).wait_recv()
                vir_on(block, plane, from_h)

    @pl.loop(0, 4)
    def _(g):
        w_now = turn_of(g)
        yl_now = (yl + g % 2) % 2

        @pl.loop(0, 8)
        def _(other):
            @pl.loop(0, 4)
            def _(t):
                @pl.when(jnp.logical_and(g < 2, jnp.logical_or(g == 1, other != side)))
                def _():
                    part = piece(other // 4, yl_now, other % 4, core, t)
                    remote(part, part, send_p.at[0, 0], recv_p.at[yl_now * 8 + other, t], partner).wait_recv()
                    to_partner(yl_now, other, t).start()

                @pl.when(g >= 2)
                def _():
                    part = piece(other // 4, yl_now, other % 4, 1 - core, t)
                    remote(part, part, send_p.at[0, 0], recv_k.at[yl_now * 8 + other, t], partner).wait_recv()

        def load(t):
            first = pl.multiple_of((4 * t + w_now) * 80, 16)
            return pltpu.make_async_copy(columns.at[pl.ds(first, 80), pl.ds(0, 1408)], coeff.at[t], own_sem.at[t])

        for t in range(4):
            load(t).start()
        for t in range(4):
            load(t).wait()
        wide = jnp.concatenate([half[i] for i in range(6)], axis=1)
        product = jnp.dot(coeff[...].reshape(320, 1408), wide, preferred_element_type=jnp.float32)
        product = product.astype(jnp.bfloat16)
        for t in range(4):
            for i in range(6):
                vir[4 * t + w_now, i // 3, i % 3] = product[80 * t : 80 * t + 80, 128 * i : 128 * i + 128]

        @pl.loop(0, 8)
        def _(n):
            v = ((x + n // 2 + 4 - z % 4) % 4) * 4 + w_now

            @pl.when(jnp.logical_not(stays(v, n % 2)))
            def _():
                vir_out(v, n % 2).start()

        @pl.when(g == 0)
        def _():
            @pl.loop(0, 4)
            def _(t):
                @pl.loop(8, 16)
                def _(e):
                    to_chip(e, t).start()

            forward(0)

    for to_h in range(2):
        for step in range(2):
            chosen[to_h, 3 * step : 3 * step + 3] = vir[plan[to_h, step], to_h]

    def column_of(to_h):
        return (pair + z + 8 * to_h) % 16

    plane_r = (pair + 32 - z - 8 * h) % 16

    def chosen_out(to_h):
        return remote(
            chosen.at[to_h], relay_r.at[h], send_w.at[to_h], recv_w.at[h], (z * 2 + to_h, column_of(to_h))
        )

    @pl.loop(0, 2)
    def _(to_h):
        @pl.when(jnp.logical_not(stays(column_of(to_h), to_h)))
        def _():
            chosen_out(to_h).start()

    @pl.loop(0, 2)
    def _(from_h):
        a = z * 2 + from_h

        def on(src):
            onward(src, q_of(paired, a), send_r.at[from_h], recv_r.at[from_h], plane_r, home_sem.at[2 + from_h])

        @pl.when(stays(plane_r, from_h))
        def _():
            on(chosen.at[h])

        @pl.when(jnp.logical_not(stays(plane_r, from_h)))
        def _():
            block = relay_r.at[from_h]
            remote(block, block, send_w.at[0], recv_w.at[from_h], partner).wait_recv()
            on(block)

    @pl.loop(1, 4)
    def _(g):
        forward(g)

    def spread(q, at_core):
        first = (q * 2 + at_core + 32 - z - 8 * h) % 16
        return paired.at[:, :, pl.ds(pl.multiple_of(first * 256, 128), 256)]

    def spread_out(e):
        part = spread(q_own, core)
        return remote(part, part, send_g.at[e], recv_g.at[q_own], (aux, ((q_own + e) % 8) * 2 + core))

    @pl.loop(0, 2)
    def _(from_h):
        part = q_of(paired, plane_r * 2 + from_h)

        @pl.when(plane_r == z)
        def _():
            pltpu.make_async_copy(chosen.at[0], part, home_sem.at[2 + from_h]).wait()

        @pl.when(plane_r != z)
        def _():
            remote(part, part, send_r.at[0], recv_r.at[from_h], partner).wait_recv()

    @pl.loop(1, 8)
    def _(e):
        spread_out(e).start()

    part = spread(q_own, core)
    remote(part, part, send_c.at[q_own], recv_c.at[q_own], partner).start()

    @pl.loop(1, 8)
    def _(e):
        q = (q_own + 8 - e) % 8
        part = spread(q, core)
        remote(part, part, send_c.at[q], recv_g.at[q], partner).wait_recv()
        remote(part, part, send_c.at[q], recv_c.at[q], partner).start()

    @pl.loop(0, 8)
    def _(q):
        part = spread(q, 1 - core)
        remote(part, part, send_c.at[q], recv_c.at[q], partner).wait()

    @pl.loop(1, 8)
    def _(e):
        spread_out(e).wait_send()

    @pl.when(owner)
    def _():
        @pl.loop(1, 16)
        def _(d):
            remote(row_part, mine(z // 4), send_z.at[d], recv_z.at[0], z_peer(d)).wait_send()

    @pl.loop(0, 4)
    def _(t):
        @pl.loop(1, 16)
        def _(e):
            to_chip(e, t).wait_send()

        @pl.loop(0, 16)
        def _(c):
            to_partner(c // 8, c % 8, t).wait_send()

    @pl.loop(0, 2)
    def _(to_h):
        @pl.when(jnp.logical_not(stays(column_of(to_h), to_h)))
        def _():
            chosen_out(to_h).wait_send()

        @pl.when(plane_r != z)
        def _():
            part = q_of(paired, 0)
            remote(chosen.at[0], part, send_r.at[to_h], recv_r.at[0], partner).wait_send()

        @pl.loop(0, 16)
        def _(v):
            @pl.when(jnp.logical_not(stays(v, to_h)))
            def _():
                vir_out(v, to_h).wait_send()

    @pl.loop(0, 16)
    def _(plane):
        @pl.loop(0, 2)
        def _(from_h):
            part = q_of(local, plane * 2 + from_h)

            @pl.when(plane == z)
            def _():
                pltpu.make_async_copy(vir.at[0, 0], part, home_sem.at[from_h]).wait()

            @pl.when(plane != z)
            def _():
                remote(vir.at[0, 0], part, send_x.at[plane, from_h], recv_x.at[plane * 2 + from_h], partner).wait()


def front(plan, rows, half):
    bf16 = jnp.bfloat16
    return pl.pallas_call(
        front_kernel,
        out_shape=(
            jax.ShapeDtypeStruct((3, 80, 4096), bf16),
            jax.ShapeDtypeStruct((6, 80, 4096), bf16),
            jax.ShapeDtypeStruct((1280, 4 * GROUP), bf16),
        ),
        in_specs=[pl.BlockSpec(memory_space=pltpu.SMEM), ANY, ANY],
        out_specs=(ANY, ANY, ANY),
        scratch_shapes=[
            pltpu.VMEM((6, 1408, 128), bf16),
            pltpu.VMEM((4, 80, 1408), bf16),
            pltpu.VMEM((16, 2, 3, 80, 128), bf16),
            pltpu.VMEM((2, 16, 3, 80, 128), bf16),
            pltpu.VMEM((2, 6, 80, 128), bf16),
            pltpu.VMEM((2, 6, 80, 128), bf16),
            DMA, DMA((4,)), DMA((4,)),
            DMA((16,)), DMA((4,)), DMA((16, 4)), DMA((16, 4)), DMA((16, 4)), DMA((16, 4)),
            DMA((16, 2)), DMA((2, 16)), DMA((2,)), DMA((2,)),
            DMA((16, 2)), DMA((32,)), DMA((2,)), DMA((2,)),
            DMA((8,)), DMA((8,)), DMA((8,)), DMA((8,)),
        ],
        compiler_params=pltpu.CompilerParams(collective_id=0, has_side_effects=True),
        name="front",
    )(plan, rows, half)


CHUNKS = 4


def density_kernel(left, right, local, paired, out, integrals, amplitudes):
    g = pl.program_id(0)
    width = local.shape[2]
    block = paired[...].reshape(480, width)

    @pl.when(g == 0)
    def _():
        integrals[...] = jnp.zeros_like(integrals)

    @pl.when(g < CHUNKS)
    def _():
        integrals[...] += lax.dot_general(
            block, local[...].reshape(240, width), (((1,), (1,)), ((), ())),
            preferred_element_type=jnp.float32,
        )

    @pl.when(g == CHUNKS - 1)
    def _():
        scaled = spin_scale * jnp.transpose(integrals[...]) / (left[...] + right[...])
        amplitudes[...] = scaled.astype(jnp.bfloat16)

    @pl.when(g >= CHUNKS)
    def _():
        rows = jnp.dot(amplitudes[...], block, preferred_element_type=jnp.float32)
        out[...] = rows.astype(jnp.bfloat16).reshape(3, 80, width)


def density_of(left, right, local, paired):
    width = 4096 // CHUNKS
    return pl.pallas_call(
        density_kernel,
        out_shape=jax.ShapeDtypeStruct((3, 80, 4096), jnp.bfloat16),
        grid=(2 * CHUNKS,),
        in_specs=[
            pl.BlockSpec((240, 1), lambda g: (0, 0)),
            pl.BlockSpec((1, 480), lambda g: (0, 0)),
            pl.BlockSpec((3, 80, width), lambda g: (0, 0, jnp.minimum(g, CHUNKS - 1))),
            pl.BlockSpec((6, 80, width), lambda g: (0, 0, g % CHUNKS)),
        ],
        out_specs=pl.BlockSpec((3, 80, width), lambda g: (0, 0, jnp.maximum(g - CHUNKS, 0))),
        scratch_shapes=[pltpu.VMEM((480, 240), jnp.float32), pltpu.VMEM((240, 480), jnp.bfloat16)],
        name="density",
    )(left, right, local, paired)


def per_device(half_ints, vir_coeffs, occ_energy, vir_energy, roster):
    aux, pair = lax.axis_index("aux"), lax.axis_index("pair")
    rows = jnp.pad(jnp.transpose(vir_coeffs), ((0, 0), (0, 4 * GROUP - vir_coeffs.shape[0])))
    plan = lax.dynamic_slice_in_dim(roster, pair * 2, 2, 0)
    local, paired, _ = front(plan, rows, half_ints)
    occ_block = lax.dynamic_slice_in_dim(occ_energy, aux * 3, 3, 0)
    vir_block = lax.dynamic_slice_in_dim(vir_energy, pair * 80, 80, 0)
    left = (vir_block[None, :] - occ_block[:, None]).reshape(240, 1)
    block_plan = lax.dynamic_index_in_dim(roster, aux, 0, keepdims=False)
    rostered = [lax.dynamic_slice_in_dim(vir_energy, block_plan[s] * 80, 80, 0) for s in range(2)]
    right = jnp.stack([r[None, :] - occ_block[:, None] for r in rostered]).reshape(1, 480)
    return jnp.transpose(density_of(left, right, local, paired), (1, 0, 2))


def solution(mesh):
    in_specs = (P("pair", None, "aux"), P(None, "aux"), P(), P(), P())
    out_specs = P("pair", "aux", None)
    return jax.shard_map(
        per_device, mesh=mesh, in_specs=in_specs, out_specs=out_specs, check_vma=False
    )
```

```python
import jax
import jax.numpy as jnp
from jax import lax
from jax.experimental import pallas as pl
from jax.experimental.pallas import tpu as pltpu
from jax.sharding import PartitionSpec as P

spin_scale = 1.3
MESH = pl.DeviceIdType.MESH
ANY = pl.BlockSpec(memory_space=pl.ANY)
DMA = pltpu.SemaphoreType.DMA

GROUP = 384


def place():
    aux, pair = lax.axis_index("aux"), lax.axis_index("pair")
    return aux // 2, aux % 2, pair // 4, (pair // 2) % 2, pair % 2, aux, pair


def remote(src, dst, send, recv, device):
    return pltpu.make_async_remote_copy(
        src_ref=src, dst_ref=dst, send_sem=send, recv_sem=recv,
        device_id=device, device_id_type=MESH,
    )


def signal(device):
    pl.semaphore_signal(
        pltpu.get_barrier_semaphore(), inc=1, device_id=device, device_id_type=MESH
    )


def front_kernel(
    roster, rows, half_hbm, local, paired, columns, half, coeff, vir, relay, chosen, relay_r,
    half_relay, half_own, vir_own, chosen_own, send_s, recv_s, send_t, recv_t, home_t,
    send_b, recv_b, send_q, recv_q, half_sem, own_sem, home_sem, send_z, recv_z, send_p, recv_p, send_k, recv_k,
    send_v, recv_v, send_w, recv_w, send_x, recv_x, send_r, recv_r, send_g, recv_g, send_c, recv_c,
):
    z, h, x, yl, core, aux, pair = place()
    w = yl * 2 + core
    side = h * 4 + x
    partner = (aux, pair + 1 - 2 * core)
    q_own = pair // 2

    half_load = pltpu.make_async_copy(half_hbm, half, half_sem)
    half_load.start()

    @pl.loop(1, 16)
    def _(d):
        signal((((z + d) % 16) * 2 + h, pair))

    @pl.loop(1, 32)
    def _(d):
        other = (h * 16 + pair + d) % 32
        signal((z * 2 + other // 16, other % 16))

    pl.semaphore_wait(pltpu.get_barrier_semaphore(), 46)

    def z_peer(d):
        return (((z + d) % 16) * 2 + h, pair)

    def piece(ch, cyl, cx, at_core, t):
        first = pl.multiple_of((8 * t + 2 * (cyl * 2 + at_core) + ch) * 40, 8)
        return columns.at[pl.ds(first, 40), pl.ds(pl.multiple_of(cx * GROUP, 128), GROUP)]

    def mine(t):
        return piece(h, yl, x, core, t)

    row_part = rows.at[:, pl.ds(pl.multiple_of(x * GROUP, 128), GROUP)]
    owner = z % 4 == w

    @pl.when(owner)
    def _():
        @pl.loop(1, 16)
        def _(d):
            remote(row_part, mine(z // 4), send_z.at[d], recv_z.at[z // 4], z_peer(d)).start()

        copy = pltpu.make_async_copy(row_part, mine(z // 4), home_sem.at[0])
        copy.start()
        copy.wait()

    def stays(v, to_h):
        return jnp.logical_and(v == pair, to_h == h)

    column = (pair + z + 8 * h) % 16

    def plane_of(from_h):
        return (pair + 32 - z - 8 * from_h) % 16

    def rows_of(c):
        return pl.ds(pl.multiple_of(c * 704, 16), 704)

    def half_out(to_h, c):
        return remote(
            half_hbm.at[3 * to_h, rows_of(c)], half_relay.at[h, rows_of(c)],
            send_s.at[to_h, c], recv_s.at[h, c], (z * 2 + to_h, column),
        )

    def half_on(src, from_h, c):
        dst = half_own.at[from_h, rows_of(c)]
        plane = plane_of(from_h)

        @pl.when(plane == z)
        def _():
            pltpu.make_async_copy(src, dst, home_t.at[from_h, c]).start()

        @pl.when(plane != z)
        def _():
            remote(src, dst, send_t.at[from_h, c], recv_t.at[from_h, c], (plane * 2 + h, pair)).start()

    @pl.loop(0, 2)
    def _(c):
        @pl.loop(0, 2)
        def _(to_h):
            @pl.when(jnp.logical_not(stays(column, to_h)))
            def _():
                half_out(to_h, c).start()

    @pl.loop(0, 2)
    def _(c):
        @pl.loop(0, 2)
        def _(from_h):
            mine_already = stays(plane_of(from_h), from_h)

            @pl.when(mine_already)
            def _():
                half_on(half_hbm.at[3 * h, rows_of(c)], from_h, c)

            @pl.when(jnp.logical_not(mine_already))
            def _():
                block = half_relay.at[from_h, rows_of(c)]
                remote(block, block, send_s.at[0, 0], recv_s.at[from_h, c], partner).wait_recv()
                half_on(block, from_h, c)

    def to_chip(e, t):
        other = (side + e) % 8
        device = (z * 2 + other // 4, (other % 4) * 4 + ((yl + e // 8) % 2) * 2 + core)
        return remote(mine(t), mine(t), send_p.at[e, t], recv_p.at[yl * 8 + side, t], device)

    def to_partner(cyl, cside, t):
        part = piece(cside // 4, cyl, cside % 4, core, t)
        return remote(part, part, send_k.at[cyl * 8 + cside, t], recv_k.at[cyl * 8 + cside, t], partner)

    @pl.loop(0, 4)
    def _(t):
        @pl.when(jnp.logical_or(jnp.logical_not(owner), t != z // 4))
        def _():
            remote(mine(t), mine(t), send_z.at[0], recv_z.at[t], partner).wait_recv()

        @pl.loop(1, 8)
        def _(e):
            to_chip(e, t).start()

        to_partner(yl, side, t).start()

    half_load.wait()

    def vir_out(v, to_h):
        return remote(
            vir.at[v, to_h], relay.at[h, pair], send_v.at[v, to_h], recv_v.at[h, pair], (z * 2 + to_h, v)
        )

    def turn_of(g):
        return (w + (1 - 2 * core) * (g // 2) + 2 * (g % 2)) % 4

    def q_of(array, a):
        return array.at[:, :, pl.ds(pl.multiple_of(a * 128, 128), 128)]

    def onward(src, dst, send, recv, plane, sem):
        @pl.when(plane == z)
        def _():
            pltpu.make_async_copy(src, dst, sem).start()

        @pl.when(plane != z)
        def _():
            remote(src, dst, send, recv, (plane * 2 + h, pair)).start()

    def vir_on(src, plane, from_h):
        a = z * 2 + from_h
        onward(src, q_of(local.at[pl.ds(1, 2)], a), send_x.at[plane, from_h], recv_x.at[a], plane, home_sem.at[from_h])

    def forward(g):
        @pl.loop(0, 8)
        def _(n):
            plane = ((x + n // 2 + z) % 4) * 4 + turn_of(g)
            from_h = n % 2

            @pl.when(stays(plane, from_h))
            def _():
                vir_on(vir.at[pair, h], plane, from_h)

            @pl.when(jnp.logical_not(stays(plane, from_h)))
            def _():
                block = relay.at[from_h, plane]
                remote(block, block, send_v.at[0, 0], recv_v.at[from_h, plane], partner).wait_recv()
                vir_on(block, plane, from_h)

    @pl.loop(0, 4)
    def _(g):
        w_now = turn_of(g)
        yl_now = (yl + g % 2) % 2

        @pl.loop(0, 8)
        def _(other):
            @pl.loop(0, 4)
            def _(t):
                @pl.when(jnp.logical_and(g < 2, jnp.logical_or(g == 1, other != side)))
                def _():
                    part = piece(other // 4, yl_now, other % 4, core, t)
                    remote(part, part, send_p.at[0, 0], recv_p.at[yl_now * 8 + other, t], partner).wait_recv()
                    to_partner(yl_now, other, t).start()

                @pl.when(g >= 2)
                def _():
                    part = piece(other // 4, yl_now, other % 4, 1 - core, t)
                    remote(part, part, send_p.at[0, 0], recv_k.at[yl_now * 8 + other, t], partner).wait_recv()

        def load(t):
            first = pl.multiple_of((4 * t + w_now) * 80, 16)
            return pltpu.make_async_copy(columns.at[pl.ds(first, 80), pl.ds(0, 1408)], coeff.at[w_now, t], own_sem.at[t])

        for t in range(4):
            load(t).start()
        for t in range(4):
            load(t).wait()
        wide = jnp.concatenate([half[i] for i in (1, 2, 4, 5)], axis=1)
        product = jnp.dot(coeff[w_now].reshape(320, 1408), wide, preferred_element_type=jnp.float32)
        product = product.astype(jnp.bfloat16)
        for t in range(4):
            for i in range(4):
                vir[4 * t + w_now, i // 2, i % 2] = product[80 * t : 80 * t + 80, 128 * i : 128 * i + 128]

        @pl.loop(0, 8)
        def _(n):
            v = ((x + n // 2 + 4 - z % 4) % 4) * 4 + w_now

            @pl.when(jnp.logical_not(stays(v, n % 2)))
            def _():
                vir_out(v, n % 2).start()

        @pl.when(g == 0)
        def _():
            @pl.loop(0, 4)
            def _(t):
                @pl.loop(8, 16)
                def _(e):
                    to_chip(e, t).start()

            forward(0)

    for to_h in range(2):
        for step in range(2):
            block = vir[roster[2 * pair + to_h, step], to_h]
            chosen[to_h, step] = block[0]
            chosen[to_h, 2 + step] = block[1]

    def late(array):
        return array.at[pl.ds(2, 4)]

    def chosen_out(to_h):
        return remote(chosen.at[to_h], relay_r.at[h], send_w.at[to_h], recv_w.at[h], (z * 2 + to_h, column))

    @pl.loop(0, 2)
    def _(to_h):
        @pl.when(jnp.logical_not(stays(column, to_h)))
        def _():
            chosen_out(to_h).start()

    @pl.loop(0, 2)
    def _(from_h):
        a = z * 2 + from_h

        def on(src):
            onward(
                src, q_of(late(paired), a), send_r.at[from_h], recv_r.at[from_h],
                plane_of(from_h), home_sem.at[2 + from_h],
            )

        @pl.when(stays(plane_of(from_h), from_h))
        def _():
            on(chosen.at[h])

        @pl.when(jnp.logical_not(stays(plane_of(from_h), from_h)))
        def _():
            block = relay_r.at[from_h]
            remote(block, block, send_w.at[0], recv_w.at[from_h], partner).wait_recv()
            on(block)

    @pl.loop(1, 4)
    def _(g):
        forward(g)

    def column_from(v, from_h):
        return ((v + 32 - z - 8 * from_h) % 16) * 2 + from_h

    @pl.loop(0, 2)
    def _(c):
        @pl.loop(0, 2)
        def _(from_h):
            dst = half_own.at[from_h, rows_of(c)]

            @pl.when(plane_of(from_h) == z)
            def _():
                pltpu.make_async_copy(half_relay.at[from_h, rows_of(c)], dst, home_t.at[from_h, c]).wait()

            @pl.when(plane_of(from_h) != z)
            def _():
                remote(dst, dst, send_t.at[0, 0], recv_t.at[from_h, c], partner).wait_recv()

    @pl.loop(0, 4)
    def _(g):
        wide = jnp.concatenate([half_own[0], half_own[1]], axis=1)
        product = jnp.dot(coeff[g].reshape(320, 1408), wide, preferred_element_type=jnp.float32)
        product = product.astype(jnp.bfloat16)
        for t in range(4):
            for i in range(2):
                vir_own[4 * t + g, i] = product[80 * t : 80 * t + 80, 128 * i : 128 * i + 128]

    for step in range(2):
        block = vir_own[roster[aux, step]]
        chosen_own[0, step] = block[0]
        chosen_own[1, step] = block[1]

    def early(array):
        return array.at[pl.ds(0, 2)]

    def own_out(d, from_h):
        v = (pair + d) % 16
        a = column_from(pair, from_h)
        block = remote(
            vir_own.at[v, from_h], q_of(local, a).at[0], send_b.at[d, from_h], recv_b.at[pair, from_h], (aux, v)
        )
        picked = remote(
            chosen_own.at[from_h], q_of(early(paired), a), send_q.at[d, from_h], recv_q.at[pair, from_h], (aux, v)
        )
        return block, picked

    def own_kept(from_h):
        a = column_from(pair, from_h)
        return (
            pltpu.make_async_copy(vir_own.at[pair, from_h], q_of(local, a).at[0], send_b.at[0, from_h]),
            pltpu.make_async_copy(chosen_own.at[from_h], q_of(early(paired), a), send_q.at[0, from_h]),
        )

    @pl.loop(0, 2)
    def _(from_h):
        for copy in own_kept(from_h):
            copy.start()

        @pl.loop(1, 16)
        def _(d):
            for copy in own_out(d, from_h):
                copy.start()

    def spread(q, at_core, from_h):
        return q_of(late(paired), column_from(q * 2 + at_core, from_h))

    def spread_out(e, from_h):
        part = spread(q_own, core, from_h)
        device = (aux, ((q_own + e) % 8) * 2 + core)
        return remote(part, part, send_g.at[e, from_h], recv_g.at[q_own, from_h], device)

    def spread_over(q, at_core, from_h):
        part = spread(q, at_core, from_h)
        return remote(part, part, send_c.at[q, from_h], recv_c.at[q, from_h], partner)

    @pl.loop(0, 2)
    def _(from_h):
        part = spread(q_own, core, from_h)

        @pl.when(plane_of(from_h) == z)
        def _():
            pltpu.make_async_copy(chosen.at[0], part, home_sem.at[2 + from_h]).wait()

        @pl.when(plane_of(from_h) != z)
        def _():
            remote(part, part, send_r.at[0], recv_r.at[from_h], partner).wait_recv()

        @pl.loop(1, 8)
        def _(e):
            spread_out(e, from_h).start()

        spread_over(q_own, core, from_h).start()

    @pl.loop(0, 2)
    def _(from_h):
        @pl.loop(1, 8)
        def _(e):
            q = (q_own + 8 - e) % 8
            part = spread(q, core, from_h)
            remote(part, part, send_c.at[q, 0], recv_g.at[q, from_h], partner).wait_recv()
            spread_over(q, core, from_h).start()

    @pl.loop(0, 2)
    def _(from_h):
        @pl.loop(0, 8)
        def _(q):
            spread_over(q, 1 - core, from_h).wait()

    @pl.loop(0, 2)
    def _(from_h):
        @pl.loop(1, 8)
        def _(e):
            spread_out(e, from_h).wait_send()

        for copy in own_kept(from_h):
            copy.wait()

        @pl.loop(1, 16)
        def _(d):
            for copy in own_out(d, from_h):
                copy.wait_send()
            v = (pair + d) % 16
            a = column_from(v, from_h)
            block, picked = q_of(local, a).at[0], q_of(early(paired), a)
            remote(block, block, send_b.at[0, 0], recv_b.at[v, from_h], partner).wait_recv()
            remote(picked, picked, send_b.at[0, 0], recv_q.at[v, from_h], partner).wait_recv()

        @pl.loop(0, 2)
        def _(c):
            @pl.when(jnp.logical_not(stays(column, from_h)))
            def _():
                half_out(from_h, c).wait_send()

            @pl.when(plane_of(from_h) != z)
            def _():
                part = half_own.at[from_h, rows_of(c)]
                remote(part, part, send_t.at[from_h, c], recv_t.at[0, 0], partner).wait_send()

    @pl.when(owner)
    def _():
        @pl.loop(1, 16)
        def _(d):
            remote(row_part, mine(z // 4), send_z.at[d], recv_z.at[0], z_peer(d)).wait_send()

    @pl.loop(0, 4)
    def _(t):
        @pl.loop(1, 16)
        def _(e):
            to_chip(e, t).wait_send()

        @pl.loop(0, 16)
        def _(c):
            to_partner(c // 8, c % 8, t).wait_send()

    @pl.loop(0, 2)
    def _(to_h):
        @pl.when(jnp.logical_not(stays(column, to_h)))
        def _():
            chosen_out(to_h).wait_send()

        @pl.when(plane_of(to_h) != z)
        def _():
            part = q_of(late(paired), 0)
            remote(chosen.at[0], part, send_r.at[to_h], recv_r.at[0], partner).wait_send()

        @pl.loop(0, 16)
        def _(v):
            @pl.when(jnp.logical_not(stays(v, to_h)))
            def _():
                vir_out(v, to_h).wait_send()

    @pl.loop(0, 16)
    def _(plane):
        @pl.loop(0, 2)
        def _(from_h):
            part = q_of(local.at[pl.ds(1, 2)], plane * 2 + from_h)

            @pl.when(plane == z)
            def _():
                pltpu.make_async_copy(vir.at[0, 0], part, home_sem.at[from_h]).wait()

            @pl.when(plane != z)
            def _():
                remote(vir.at[0, 0], part, send_x.at[plane, from_h], recv_x.at[plane * 2 + from_h], partner).wait()


def front(roster, rows, half):
    bf16 = jnp.bfloat16
    return pl.pallas_call(
        front_kernel,
        out_shape=(
            jax.ShapeDtypeStruct((3, 80, 4096), bf16),
            jax.ShapeDtypeStruct((6, 80, 4096), bf16),
            jax.ShapeDtypeStruct((1280, 4 * GROUP), bf16),
        ),
        in_specs=[pl.BlockSpec(memory_space=pltpu.SMEM), ANY, ANY],
        out_specs=(ANY, ANY, ANY),
        scratch_shapes=[
            pltpu.VMEM((6, 1408, 128), bf16),
            pltpu.VMEM((4, 4, 80, 1408), bf16),
            pltpu.VMEM((16, 2, 2, 80, 128), bf16),
            pltpu.VMEM((2, 16, 2, 80, 128), bf16),
            pltpu.VMEM((2, 4, 80, 128), bf16),
            pltpu.VMEM((2, 4, 80, 128), bf16),
            pltpu.VMEM((2, 1408, 128), bf16),
            pltpu.VMEM((2, 1408, 128), bf16),
            pltpu.VMEM((16, 2, 80, 128), bf16),
            pltpu.VMEM((2, 2, 80, 128), bf16),
            DMA((2, 2)), DMA((2, 2)), DMA((2, 2)), DMA((2, 2)), DMA((2, 2)),
            DMA((16, 2)), DMA((16, 2)), DMA((16, 2)), DMA((16, 2)),
            DMA, DMA((4,)), DMA((4,)),
            DMA((16,)), DMA((4,)), DMA((16, 4)), DMA((16, 4)), DMA((16, 4)), DMA((16, 4)),
            DMA((16, 2)), DMA((2, 16)), DMA((2,)), DMA((2,)),
            DMA((16, 2)), DMA((32,)), DMA((2,)), DMA((2,)),
            DMA((8, 2)), DMA((8, 2)), DMA((8, 2)), DMA((8, 2)),
        ],
        compiler_params=pltpu.CompilerParams(collective_id=0, has_side_effects=True),
        name="front",
    )(roster, rows, half)


CHUNKS = 4


def density_kernel(left, right, local, paired, out, integrals, amplitudes):
    g = pl.program_id(0)
    width = local.shape[2]
    block = paired[...].reshape(480, width)

    @pl.when(g == 0)
    def _():
        integrals[...] = jnp.zeros_like(integrals)

    @pl.when(g < CHUNKS)
    def _():
        integrals[...] += lax.dot_general(
            block, local[...].reshape(240, width), (((1,), (1,)), ((), ())),
            preferred_element_type=jnp.float32,
        )

    @pl.when(g == CHUNKS - 1)
    def _():
        scaled = spin_scale * jnp.transpose(integrals[...]) / (left[...] + right[...])
        amplitudes[...] = scaled.astype(jnp.bfloat16)

    @pl.when(g >= CHUNKS)
    def _():
        rows = jnp.dot(amplitudes[...], block, preferred_element_type=jnp.float32)
        out[...] = rows.astype(jnp.bfloat16).reshape(3, 80, width)


def density_of(left, right, local, paired):
    width = 4096 // CHUNKS
    return pl.pallas_call(
        density_kernel,
        out_shape=jax.ShapeDtypeStruct((3, 80, 4096), jnp.bfloat16),
        grid=(2 * CHUNKS,),
        in_specs=[
            pl.BlockSpec((240, 1), lambda g: (0, 0)),
            pl.BlockSpec((1, 480), lambda g: (0, 0)),
            pl.BlockSpec((3, 80, width), lambda g: (0, 0, jnp.minimum(g, CHUNKS - 1))),
            pl.BlockSpec((6, 80, width), lambda g: (0, 0, g % CHUNKS)),
        ],
        out_specs=pl.BlockSpec((3, 80, width), lambda g: (0, 0, jnp.maximum(g - CHUNKS, 0))),
        scratch_shapes=[pltpu.VMEM((480, 240), jnp.float32), pltpu.VMEM((240, 480), jnp.bfloat16)],
        name="density",
    )(left, right, local, paired)


def per_device(half_ints, vir_coeffs, occ_energy, vir_energy, roster):
    aux, pair = lax.axis_index("aux"), lax.axis_index("pair")
    rows = jnp.pad(jnp.transpose(vir_coeffs), ((0, 0), (0, 4 * GROUP - vir_coeffs.shape[0])))
    local, paired, _ = front(roster, rows, half_ints)
    occ_block = lax.dynamic_slice_in_dim(occ_energy, aux * 3, 3, 0)
    vir_block = lax.dynamic_slice_in_dim(vir_energy, pair * 80, 80, 0)
    left = (vir_block[None, :] - occ_block[:, None]).reshape(240, 1)
    block_plan = lax.dynamic_index_in_dim(roster, aux, 0, keepdims=False)
    rostered = [lax.dynamic_slice_in_dim(vir_energy, block_plan[s] * 80, 80, 0) for s in range(2)]
    right = (jnp.stack(rostered)[None] - occ_block[:, None, None]).reshape(1, 480)
    return jnp.transpose(density_of(left, right, local, paired), (1, 0, 2))


def solution(mesh):
    in_specs = (P("pair", None, "aux"), P(None, "aux"), P(), P(), P())
    out_specs = P("pair", "aux", None)
    return jax.shard_map(
        per_device, mesh=mesh, in_specs=in_specs, out_specs=out_specs, check_vma=False
    )
```

```python
import jax
import jax.numpy as jnp
from jax import lax
from jax.experimental import pallas as pl
from jax.experimental.pallas import tpu as pltpu
from jax.sharding import PartitionSpec as P

spin_scale = 1.3
MESH = pl.DeviceIdType.MESH
ANY = pl.BlockSpec(memory_space=pl.ANY)
DMA = pltpu.SemaphoreType.DMA

GROUP = 384


def place():
    aux, pair = lax.axis_index("aux"), lax.axis_index("pair")
    return aux // 2, aux % 2, pair // 4, (pair // 2) % 2, pair % 2, aux, pair


def remote(src, dst, send, recv, device):
    return pltpu.make_async_remote_copy(
        src_ref=src, dst_ref=dst, send_sem=send, recv_sem=recv,
        device_id=device, device_id_type=MESH,
    )


def signal(device):
    pl.semaphore_signal(
        pltpu.get_barrier_semaphore(), inc=1, device_id=device, device_id_type=MESH
    )


def front_kernel(
    roster, rows_hbm, half_hbm, local, paired, columns, rows, half, coeff, vir, relay, chosen, relay_r,
    half_relay, half_own, vir_own, chosen_own, send_s, recv_s, send_t, recv_t, home_t,
    send_b, recv_b, send_q, recv_q, half_sem, own_sem, home_sem, send_z, recv_z, send_p, recv_p, send_k, recv_k,
    send_v, recv_v, send_w, recv_w, send_x, recv_x, send_r, recv_r, send_g, recv_g, send_c, recv_c,
):
    z, h, x, yl, core, aux, pair = place()
    w = yl * 2 + core
    side = h * 4 + x
    partner = (aux, pair + 1 - 2 * core)
    q_own = pair // 2

    half_load = pltpu.make_async_copy(half_hbm, half, half_sem)
    half_load.start()
    rows_load = pltpu.make_async_copy(rows_hbm, rows.at[:, pl.ds(0, 1408)], home_sem.at[0])
    rows_load.start()
    rows[:, 1408:] = jnp.zeros((40, 4 * GROUP - 1408), jnp.bfloat16)

    @pl.loop(1, 16)
    def _(d):
        signal((((z + d) % 16) * 2 + h, pair))

    @pl.loop(1, 32)
    def _(d):
        other = (h * 16 + pair + d) % 32
        signal((z * 2 + other // 16, other % 16))

    rows_load.wait()
    pl.semaphore_wait(pltpu.get_barrier_semaphore(), 46)

    def z_peer(d):
        return (((z + d) % 16) * 2 + h, pair)

    def piece(ch, cyl, cx, at_core, t):
        first = pl.multiple_of((8 * t + 2 * (cyl * 2 + at_core) + ch) * 40, 8)
        return columns.at[pl.ds(first, 40), pl.ds(pl.multiple_of(cx * GROUP, 128), GROUP)]

    def mine(t):
        return piece(h, yl, x, core, t)

    row_part = rows.at[:, pl.ds(pl.multiple_of(x * GROUP, 128), GROUP)]
    owner = z % 4 == w

    @pl.when(owner)
    def _():
        @pl.loop(1, 16)
        def _(d):
            remote(row_part, mine(z // 4), send_z.at[d], recv_z.at[z // 4], z_peer(d)).start()

        copy = pltpu.make_async_copy(row_part, mine(z // 4), home_sem.at[0])
        copy.start()
        copy.wait()

    def stays(v, to_h):
        return jnp.logical_and(v == pair, to_h == h)

    column = (pair + z + 8 * h) % 16

    def plane_of(from_h):
        return (pair + 32 - z - 8 * from_h) % 16

    def rows_of(c):
        return pl.ds(pl.multiple_of(c * 704, 16), 704)

    def half_out(to_h, c):
        return remote(
            half_hbm.at[3 * to_h, rows_of(c)], half_relay.at[h, rows_of(c)],
            send_s.at[to_h, c], recv_s.at[h, c], (z * 2 + to_h, column),
        )

    def half_on(src, from_h, c):
        dst = half_own.at[from_h, rows_of(c)]
        plane = plane_of(from_h)

        @pl.when(plane == z)
        def _():
            pltpu.make_async_copy(src, dst, home_t.at[from_h, c]).start()

        @pl.when(plane != z)
        def _():
            remote(src, dst, send_t.at[from_h, c], recv_t.at[from_h, c], (plane * 2 + h, pair)).start()

    @pl.loop(0, 2)
    def _(c):
        @pl.loop(0, 2)
        def _(to_h):
            @pl.when(jnp.logical_not(stays(column, to_h)))
            def _():
                half_out(to_h, c).start()

    @pl.loop(0, 2)
    def _(c):
        @pl.loop(0, 2)
        def _(from_h):
            mine_already = stays(plane_of(from_h), from_h)

            @pl.when(mine_already)
            def _():
                half_on(half_hbm.at[3 * h, rows_of(c)], from_h, c)

            @pl.when(jnp.logical_not(mine_already))
            def _():
                block = half_relay.at[from_h, rows_of(c)]
                remote(block, block, send_s.at[0, 0], recv_s.at[from_h, c], partner).wait_recv()
                half_on(block, from_h, c)

    def to_chip(e, t):
        other = (side + e) % 8
        device = (z * 2 + other // 4, (other % 4) * 4 + ((yl + e // 8) % 2) * 2 + core)
        return remote(mine(t), mine(t), send_p.at[e, t], recv_p.at[yl * 8 + side, t], device)

    def to_partner(cyl, cside, t):
        part = piece(cside // 4, cyl, cside % 4, core, t)
        return remote(part, part, send_k.at[cyl * 8 + cside, t], recv_k.at[cyl * 8 + cside, t], partner)

    @pl.loop(0, 4)
    def _(t):
        @pl.when(jnp.logical_or(jnp.logical_not(owner), t != z // 4))
        def _():
            remote(mine(t), mine(t), send_z.at[0], recv_z.at[t], partner).wait_recv()

        @pl.loop(1, 8)
        def _(e):
            to_chip(e, t).start()

        to_partner(yl, side, t).start()

    half_load.wait()

    def vir_out(v, to_h):
        return remote(
            vir.at[v, to_h], relay.at[h, pair], send_v.at[v, to_h], recv_v.at[h, pair], (z * 2 + to_h, v)
        )

    def turn_of(g):
        return (w + (1 - 2 * core) * (g // 2) + 2 * (g % 2)) % 4

    def q_of(array, a):
        return array.at[:, :, pl.ds(pl.multiple_of(a * 128, 128), 128)]

    def onward(src, dst, send, recv, plane, sem):
        @pl.when(plane == z)
        def _():
            pltpu.make_async_copy(src, dst, sem).start()

        @pl.when(plane != z)
        def _():
            remote(src, dst, send, recv, (plane * 2 + h, pair)).start()

    def vir_on(src, plane, from_h):
        a = z * 2 + from_h
        onward(src, q_of(local.at[pl.ds(1, 2)], a), send_x.at[plane, from_h], recv_x.at[a], plane, home_sem.at[from_h])

    def forward(g):
        @pl.loop(0, 8)
        def _(n):
            plane = ((x + n // 2 + z) % 4) * 4 + turn_of(g)
            from_h = n % 2

            @pl.when(stays(plane, from_h))
            def _():
                vir_on(vir.at[pair, h], plane, from_h)

            @pl.when(jnp.logical_not(stays(plane, from_h)))
            def _():
                block = relay.at[from_h, plane]
                remote(block, block, send_v.at[0, 0], recv_v.at[from_h, plane], partner).wait_recv()
                vir_on(block, plane, from_h)

    @pl.loop(0, 4)
    def _(g):
        w_now = turn_of(g)
        yl_now = (yl + g % 2) % 2

        @pl.loop(0, 8)
        def _(other):
            @pl.loop(0, 4)
            def _(t):
                @pl.when(jnp.logical_and(g < 2, jnp.logical_or(g == 1, other != side)))
                def _():
                    part = piece(other // 4, yl_now, other % 4, core, t)
                    remote(part, part, send_p.at[0, 0], recv_p.at[yl_now * 8 + other, t], partner).wait_recv()
                    to_partner(yl_now, other, t).start()

                @pl.when(g >= 2)
                def _():
                    part = piece(other // 4, yl_now, other % 4, 1 - core, t)
                    remote(part, part, send_p.at[0, 0], recv_k.at[yl_now * 8 + other, t], partner).wait_recv()

        def load(t):
            first = pl.multiple_of((4 * t + w_now) * 80, 16)
            return pltpu.make_async_copy(columns.at[pl.ds(first, 80), pl.ds(0, 1408)], coeff.at[w_now, t], own_sem.at[t])

        for t in range(4):
            load(t).start()
        for t in range(4):
            load(t).wait()
        wide = jnp.concatenate([half[i] for i in (1, 2, 4, 5)], axis=1)
        product = jnp.dot(coeff[w_now].reshape(320, 1408), wide, preferred_element_type=jnp.float32)
        product = product.astype(jnp.bfloat16)
        for t in range(4):
            for i in range(4):
                vir[4 * t + w_now, i // 2, i % 2] = product[80 * t : 80 * t + 80, 128 * i : 128 * i + 128]

        @pl.loop(0, 8)
        def _(n):
            v = ((x + n // 2 + 4 - z % 4) % 4) * 4 + w_now

            @pl.when(jnp.logical_not(stays(v, n % 2)))
            def _():
                vir_out(v, n % 2).start()

        @pl.when(g == 0)
        def _():
            @pl.loop(0, 4)
            def _(t):
                @pl.loop(8, 16)
                def _(e):
                    to_chip(e, t).start()

            forward(0)

    for to_h in range(2):
        for step in range(2):
            block = vir[roster[step, 2 * pair + to_h], to_h]
            chosen[to_h, step] = block[0]
            chosen[to_h, 2 + step] = block[1]

    def late(array):
        return array.at[pl.ds(2, 4)]

    def chosen_out(to_h):
        return remote(chosen.at[to_h], relay_r.at[h], send_w.at[to_h], recv_w.at[h], (z * 2 + to_h, column))

    @pl.loop(0, 2)
    def _(to_h):
        @pl.when(jnp.logical_not(stays(column, to_h)))
        def _():
            chosen_out(to_h).start()

    @pl.loop(0, 2)
    def _(from_h):
        a = z * 2 + from_h

        def on(src):
            onward(
                src, q_of(late(paired), a), send_r.at[from_h], recv_r.at[from_h],
                plane_of(from_h), home_sem.at[2 + from_h],
            )

        @pl.when(stays(plane_of(from_h), from_h))
        def _():
            on(chosen.at[h])

        @pl.when(jnp.logical_not(stays(plane_of(from_h), from_h)))
        def _():
            block = relay_r.at[from_h]
            remote(block, block, send_w.at[0], recv_w.at[from_h], partner).wait_recv()
            on(block)

    @pl.loop(1, 4)
    def _(g):
        forward(g)

    def column_from(v, from_h):
        return ((v + 32 - z - 8 * from_h) % 16) * 2 + from_h

    @pl.loop(0, 2)
    def _(c):
        @pl.loop(0, 2)
        def _(from_h):
            dst = half_own.at[from_h, rows_of(c)]

            @pl.when(plane_of(from_h) == z)
            def _():
                pltpu.make_async_copy(half_relay.at[from_h, rows_of(c)], dst, home_t.at[from_h, c]).wait()

            @pl.when(plane_of(from_h) != z)
            def _():
                remote(dst, dst, send_t.at[0, 0], recv_t.at[from_h, c], partner).wait_recv()

    @pl.loop(0, 4)
    def _(g):
        wide = jnp.concatenate([half_own[0], half_own[1]], axis=1)
        product = jnp.dot(coeff[g].reshape(320, 1408), wide, preferred_element_type=jnp.float32)
        product = product.astype(jnp.bfloat16)
        for t in range(4):
            for i in range(2):
                vir_own[4 * t + g, i] = product[80 * t : 80 * t + 80, 128 * i : 128 * i + 128]

    for step in range(2):
        block = vir_own[roster[step, aux]]
        chosen_own[0, step] = block[0]
        chosen_own[1, step] = block[1]

    def early(array):
        return array.at[pl.ds(0, 2)]

    def own_out(d, from_h):
        v = (pair + d) % 16
        a = column_from(pair, from_h)
        block = remote(
            vir_own.at[v, from_h], q_of(local, a).at[0], send_b.at[d, from_h], recv_b.at[pair, from_h], (aux, v)
        )
        picked = remote(
            chosen_own.at[from_h], q_of(early(paired), a), send_q.at[d, from_h], recv_q.at[pair, from_h], (aux, v)
        )
        return block, picked

    def own_kept(from_h):
        a = column_from(pair, from_h)
        return (
            pltpu.make_async_copy(vir_own.at[pair, from_h], q_of(local, a).at[0], send_b.at[0, from_h]),
            pltpu.make_async_copy(chosen_own.at[from_h], q_of(early(paired), a), send_q.at[0, from_h]),
        )

    @pl.loop(0, 2)
    def _(from_h):
        for copy in own_kept(from_h):
            copy.start()

        @pl.loop(1, 16)
        def _(d):
            for copy in own_out(d, from_h):
                copy.start()

    def spread(q, at_core, from_h):
        return q_of(late(paired), column_from(q * 2 + at_core, from_h))

    def spread_out(e, from_h):
        part = spread(q_own, core, from_h)
        device = (aux, ((q_own + e) % 8) * 2 + core)
        return remote(part, part, send_g.at[e, from_h], recv_g.at[q_own, from_h], device)

    def spread_over(q, at_core, from_h):
        part = spread(q, at_core, from_h)
        return remote(part, part, send_c.at[q, from_h], recv_c.at[q, from_h], partner)

    @pl.loop(0, 2)
    def _(from_h):
        part = spread(q_own, core, from_h)

        @pl.when(plane_of(from_h) == z)
        def _():
            pltpu.make_async_copy(chosen.at[0], part, home_sem.at[2 + from_h]).wait()

        @pl.when(plane_of(from_h) != z)
        def _():
            remote(part, part, send_r.at[0], recv_r.at[from_h], partner).wait_recv()

        @pl.loop(1, 8)
        def _(e):
            spread_out(e, from_h).start()

        spread_over(q_own, core, from_h).start()

    @pl.loop(0, 2)
    def _(from_h):
        @pl.loop(1, 8)
        def _(e):
            q = (q_own + 8 - e) % 8
            part = spread(q, core, from_h)
            remote(part, part, send_c.at[q, 0], recv_g.at[q, from_h], partner).wait_recv()
            spread_over(q, core, from_h).start()

    @pl.loop(0, 2)
    def _(from_h):
        @pl.loop(0, 8)
        def _(q):
            spread_over(q, 1 - core, from_h).wait()

    @pl.loop(0, 2)
    def _(from_h):
        @pl.loop(1, 8)
        def _(e):
            spread_out(e, from_h).wait_send()

        for copy in own_kept(from_h):
            copy.wait()

        @pl.loop(1, 16)
        def _(d):
            for copy in own_out(d, from_h):
                copy.wait_send()
            v = (pair + d) % 16
            a = column_from(v, from_h)
            block, picked = q_of(local, a).at[0], q_of(early(paired), a)
            remote(block, block, send_b.at[0, 0], recv_b.at[v, from_h], partner).wait_recv()
            remote(picked, picked, send_b.at[0, 0], recv_q.at[v, from_h], partner).wait_recv()

        @pl.loop(0, 2)
        def _(c):
            @pl.when(jnp.logical_not(stays(column, from_h)))
            def _():
                half_out(from_h, c).wait_send()

            @pl.when(plane_of(from_h) != z)
            def _():
                part = half_own.at[from_h, rows_of(c)]
                remote(part, part, send_t.at[from_h, c], recv_t.at[0, 0], partner).wait_send()

    @pl.when(owner)
    def _():
        @pl.loop(1, 16)
        def _(d):
            remote(row_part, mine(z // 4), send_z.at[d], recv_z.at[0], z_peer(d)).wait_send()

    @pl.loop(0, 4)
    def _(t):
        @pl.loop(1, 16)
        def _(e):
            to_chip(e, t).wait_send()

        @pl.loop(0, 16)
        def _(c):
            to_partner(c // 8, c % 8, t).wait_send()

    @pl.loop(0, 2)
    def _(to_h):
        @pl.when(jnp.logical_not(stays(column, to_h)))
        def _():
            chosen_out(to_h).wait_send()

        @pl.when(plane_of(to_h) != z)
        def _():
            part = q_of(late(paired), 0)
            remote(chosen.at[0], part, send_r.at[to_h], recv_r.at[0], partner).wait_send()

        @pl.loop(0, 16)
        def _(v):
            @pl.when(jnp.logical_not(stays(v, to_h)))
            def _():
                vir_out(v, to_h).wait_send()

    @pl.loop(0, 16)
    def _(plane):
        @pl.loop(0, 2)
        def _(from_h):
            part = q_of(local.at[pl.ds(1, 2)], plane * 2 + from_h)

            @pl.when(plane == z)
            def _():
                pltpu.make_async_copy(vir.at[0, 0], part, home_sem.at[from_h]).wait()

            @pl.when(plane != z)
            def _():
                remote(vir.at[0, 0], part, send_x.at[plane, from_h], recv_x.at[plane * 2 + from_h], partner).wait()


def front(roster, rows, half):
    bf16 = jnp.bfloat16
    return pl.pallas_call(
        front_kernel,
        out_shape=(
            jax.ShapeDtypeStruct((3, 80, 4096), bf16),
            jax.ShapeDtypeStruct((6, 80, 4096), bf16),
            jax.ShapeDtypeStruct((1280, 4 * GROUP), bf16),
        ),
        in_specs=[pl.BlockSpec(memory_space=pltpu.SMEM), ANY, ANY],
        out_specs=(ANY, ANY, ANY),
        scratch_shapes=[
            pltpu.VMEM((40, 4 * GROUP), bf16),
            pltpu.VMEM((6, 1408, 128), bf16),
            pltpu.VMEM((4, 4, 80, 1408), bf16),
            pltpu.VMEM((16, 2, 2, 80, 128), bf16),
            pltpu.VMEM((2, 16, 2, 80, 128), bf16),
            pltpu.VMEM((2, 4, 80, 128), bf16),
            pltpu.VMEM((2, 4, 80, 128), bf16),
            pltpu.VMEM((2, 1408, 128), bf16),
            pltpu.VMEM((2, 1408, 128), bf16),
            pltpu.VMEM((16, 2, 80, 128), bf16),
            pltpu.VMEM((2, 2, 80, 128), bf16),
            DMA((2, 2)), DMA((2, 2)), DMA((2, 2)), DMA((2, 2)), DMA((2, 2)),
            DMA((16, 2)), DMA((16, 2)), DMA((16, 2)), DMA((16, 2)),
            DMA, DMA((4,)), DMA((4,)),
            DMA((16,)), DMA((4,)), DMA((16, 4)), DMA((16, 4)), DMA((16, 4)), DMA((16, 4)),
            DMA((16, 2)), DMA((2, 16)), DMA((2,)), DMA((2,)),
            DMA((16, 2)), DMA((32,)), DMA((2,)), DMA((2,)),
            DMA((8, 2)), DMA((8, 2)), DMA((8, 2)), DMA((8, 2)),
        ],
        compiler_params=pltpu.CompilerParams(collective_id=0, has_side_effects=True),
        name="front",
    )(roster, rows, half)


CHUNKS = 2


def density_kernel(left, right, local, paired, out, integrals, amplitudes):
    g = pl.program_id(0)
    width = local.shape[2]
    block = paired[...].reshape(480, width)

    @pl.when(g == 0)
    def _():
        integrals[...] = jnp.zeros_like(integrals)

    @pl.when(g < CHUNKS)
    def _():
        integrals[...] += lax.dot_general(
            block, local[...].reshape(240, width), (((1,), (1,)), ((), ())),
            preferred_element_type=jnp.float32,
        )

    @pl.when(g == CHUNKS - 1)
    def _():
        scaled = spin_scale * jnp.transpose(integrals[...]) / (left[...] + right[...])
        amplitudes[...] = scaled.astype(jnp.bfloat16)

    @pl.when(g >= CHUNKS)
    def _():
        rows = jnp.dot(amplitudes[...], block, preferred_element_type=jnp.float32)
        out[...] = rows.astype(jnp.bfloat16).reshape(3, 80, width)


def density_of(left, right, local, paired):
    width = 4096 // CHUNKS
    return pl.pallas_call(
        density_kernel,
        out_shape=jax.ShapeDtypeStruct((3, 80, 4096), jnp.bfloat16),
        grid=(2 * CHUNKS,),
        in_specs=[
            pl.BlockSpec((240, 1), lambda g: (0, 0)),
            pl.BlockSpec((1, 480), lambda g: (0, 0)),
            pl.BlockSpec((3, 80, width), lambda g: (0, 0, jnp.minimum(g, CHUNKS - 1))),
            pl.BlockSpec((6, 80, width), lambda g: (0, 0, g % CHUNKS)),
        ],
        out_specs=pl.BlockSpec((3, 80, width), lambda g: (0, 0, jnp.maximum(g - CHUNKS, 0))),
        scratch_shapes=[pltpu.VMEM((480, 240), jnp.float32), pltpu.VMEM((240, 480), jnp.bfloat16)],
        name="density",
    )(left, right, local, paired)


def per_device(half_ints, vir_coeffs, occ_energy, vir_energy, roster):
    aux, pair = lax.axis_index("aux"), lax.axis_index("pair")
    rows = jnp.transpose(vir_coeffs)
    local, paired, _ = front(jnp.transpose(roster), rows, half_ints)
    occ_block = lax.dynamic_slice_in_dim(occ_energy, aux * 3, 3, 0)
    vir_block = lax.dynamic_slice_in_dim(vir_energy, pair * 80, 80, 0)
    left = (vir_block[None, :] - occ_block[:, None]).reshape(240, 1)
    block_plan = lax.dynamic_index_in_dim(roster, aux, 0, keepdims=False)
    rostered = [lax.dynamic_slice_in_dim(vir_energy, block_plan[s] * 80, 80, 0) for s in range(2)]
    right = (jnp.stack(rostered)[None] - occ_block[:, None, None]).reshape(1, 480)
    return jnp.transpose(density_of(left, right, local, paired), (1, 0, 2))


def solution(mesh):
    in_specs = (P("pair", None, "aux"), P(None, "aux"), P(), P(), P())
    out_specs = P("pair", "aux", None)
    return jax.shard_map(
        per_device, mesh=mesh, in_specs=in_specs, out_specs=out_specs, check_vma=False
    )
```
